32 devices in a mesh: row: 2 (over x), col: 4 (over y, core), mode: 4 (over z).
Axes of the slice: x: 2, y: 2, z: 4, core: 2. Of those that a mesh axis runs over, the one named last changes fastest.
Arguments:
- object_field: float32 [2, 512, 1024], P(None, 'row', 'col'), may hold values from -6 to 6
- probe_real: float32 [4, 128, 128], P('mode'), may hold values from -3 to 3
- probe_imag: float32 [4, 128, 128], P('mode'), may hold values from -3 to 3
- amplitude: float32 [2, 4, 8, 128, 128], P('row', 'col'), may hold values from 0 to 3
- positions: int32 [2, 4, 8, 2], P('row', 'col'), may hold values from 0 to 256, as said below
- counts: int32 [2, 4], P('row', 'col'), may hold values from 2 to 8, as said below
Outputs:
- updated: float32 [2, 512, 1024], P(None, 'row', 'col')
The draws below stay inside these ranges and needn't reach their ends.
Inputs may be any that keep to these rules, and one draw needn't show every extreme that they name: `positions`: offsets lie in 0 to 256 for rows and 0 to 256 for columns. In every tile slot 0 starts within the first 64 rows and columns of the window, and slot 1 ends within the last 64 rows and columns. `counts`: some tile has 8 frames and some tile has 2.
All inputs are finite; a program needn't handle non-finite values.
Results may differ from the reference program's by a relative error of at most 0.0003.
Values sent between devices are 32-bit elements; how exact they have to be, the bound alone decides.
A program may use at most 64 MiB of HBM per device.

```python
import jax
import jax.numpy as jnp
from jax import lax

FRAME = 128
MARGIN = 64
SLOTS = 8
TH = 256
TW = 256
MODES = 4
NH = 512
NW = 1024
N_ROW = 2
N_COL = 4


def draw_positions(key, part):
    tiles = NH // TH * (NW // TW)
    span_rows = TH + 2 * MARGIN - FRAME
    span_cols = TW + 2 * MARGIN - FRAME
    keys = jax.random.split(jax.random.fold_in(key, 11), 6)
    rows = jax.random.randint(keys[0], (tiles, SLOTS), 0, span_rows + 1)
    cols = jax.random.randint(keys[1], (tiles, SLOTS), 0, span_cols + 1)
    rows = rows.at[:, 0].set(jax.random.randint(keys[2], (tiles,), 0, MARGIN))
    cols = cols.at[:, 0].set(jax.random.randint(keys[3], (tiles,), 0, MARGIN))
    rows = rows.at[:, 1].set(jax.random.randint(keys[4], (tiles,), span_rows - MARGIN + 1, span_rows + 1))
    cols = cols.at[:, 1].set(jax.random.randint(keys[5], (tiles,), span_cols - MARGIN + 1, span_cols + 1))
    stacked = jnp.stack([rows, cols], axis=-1).astype(jnp.int32)
    return stacked.reshape(NH // TH, NW // TW, SLOTS, 2)


def draw_counts(key, part):
    tiles = NH // TH * (NW // TW)
    keys = jax.random.split(jax.random.fold_in(key, 23), 3)
    first = jax.random.randint(keys[0], (tiles,), 0, SLOTS - 1)
    second = jax.random.randint(keys[1], (tiles,), 0, SLOTS - 1)
    values = 2 + jnp.minimum(first, second)
    chosen = jax.random.randint(keys[2], (), 0, tiles)
    values = values.at[chosen].set(SLOTS)
    values = values.at[(chosen + 1) % tiles].set(2)
    return values.astype(jnp.int32).reshape(NH // TH, NW // TW)


def block_scale(key, dims, cuts, smallest, top_value):
    def one(dim, parts):
        heights = jax.random.uniform(jax.random.fold_in(jax.random.fold_in(key, 6), dim), (parts,), jnp.float32, smallest / len(cuts), top_value / len(cuts))
        return jnp.repeat(jnp.exp(heights), dims[dim] // parts).reshape((-1,) + (1,) * (len(dims) - dim - 1))

    gain = one(*cuts[0])
    for cut in cuts[1:]:
        gain = gain * one(*cut)
    return gain


def noise(rng, extent, deviation, limit, pieces=(), kind=jnp.bfloat16):
    result = deviation * jax.random.normal(rng, extent, jnp.float32)
    if pieces:
        result = result * block_scale(rng, extent, pieces, -0.22, 0.18)
    return jnp.clip(result, -limit, limit).astype(kind)


def setup_inputs(seed: int = 0) -> dict:
    key_of = jax.random.split(jax.random.key(seed), 7)
    object_field = noise(key_of[0], (2, NH, NW), 1.0, 6.0, ((1, 2), (2, 4)), jnp.float32)
    probe_real = noise(key_of[1], (MODES, FRAME, FRAME), 0.5, 3.0, ((0, 4),), jnp.float32)
    probe_imag = noise(key_of[2], (MODES, FRAME, FRAME), 0.5, 3.0, ((0, 4),), jnp.float32)
    amplitude = jnp.clip(3.0 * jax.random.uniform(key_of[3], (N_ROW, N_COL, SLOTS, FRAME, FRAME), jnp.float32) ** block_scale(key_of[3], (N_ROW, N_COL, SLOTS, FRAME, FRAME), ((0, 2), (1, 4)), -0.2, 0.2), 0.0, 3.0)
    positions = draw_positions(jax.random.fold_in(key_of[6], 71), 0)
    counts = draw_counts(jax.random.fold_in(key_of[6], 71), 0)
    return {"object_field": object_field, "probe_real": probe_real, "probe_imag": probe_imag, "amplitude": amplitude, "positions": positions, "counts": counts}


STEP_SIZE = 0.25

def reference(object_field, probe_real, probe_imag, amplitude, positions, counts):
    ext_rows = TH + 2 * MARGIN
    ext_cols = TW + 2 * MARGIN
    padded = jnp.pad(object_field, ((0, 0), (MARGIN, MARGIN), (MARGIN, MARGIN)))
    probe = lax.complex(probe_real, probe_imag)
    anchor = jnp.zeros((), jnp.int32)

    def frame_grad(window, offset, target):
        patch = lax.dynamic_slice(window, (anchor, offset[0], offset[1]), (2, FRAME, FRAME))
        exit_wave = probe * lax.complex(patch[0], patch[1])
        spectra = jnp.fft.fft2(exit_wave, norm='ortho')
        intensity = lax.optimization_barrier(jnp.sum(jnp.real(spectra) ** 2 + jnp.imag(spectra) ** 2, axis=0))
        keep = 1.0 - target / jnp.maximum(jnp.sqrt(intensity), 1.0)
        back = jnp.fft.ifft2(spectra * keep, norm='ortho')
        contrib = lax.optimization_barrier(jnp.sum(jnp.conj(probe) * back, axis=0))
        return jnp.stack([jnp.real(contrib), jnp.imag(contrib)])

    def tile_step(gradient, index):
        row_tile = index // N_COL
        col_tile = index % N_COL
        start = (anchor, row_tile * TH, col_tile * TW)
        window = lax.dynamic_slice(padded, start, (2, ext_rows, ext_cols))
        local = jnp.zeros((2, ext_rows, ext_cols), padded.dtype)

        def slot_step(slot, local):
            offset = positions[row_tile, col_tile, slot].astype(jnp.int32)
            weight = (slot < counts[row_tile, col_tile]).astype(padded.dtype)
            piece = frame_grad(window, offset, amplitude[row_tile, col_tile, slot]) * weight
            corner = (anchor, offset[0], offset[1])
            previous = lax.dynamic_slice(local, corner, (2, FRAME, FRAME))
            return lax.dynamic_update_slice(local, previous + piece, corner)
        local = lax.fori_loop(0, SLOTS, slot_step, local)
        previous = lax.dynamic_slice(gradient, start, (2, ext_rows, ext_cols))
        return (lax.dynamic_update_slice(gradient, previous + local, start), None)
    gradient, _ = lax.scan(tile_step, jnp.zeros(padded.shape, padded.dtype), jnp.arange(N_ROW * N_COL, dtype=jnp.int32))
    cropped = gradient[:, MARGIN:MARGIN + NH, MARGIN:MARGIN + NW]
    return object_field - STEP_SIZE * cropped
```

```python
import functools

import jax
import jax.numpy as jnp
import numpy as np
from jax import lax
from jax.experimental import pallas as pl
from jax.experimental.pallas import tpu as pltpu
from jax.sharding import PartitionSpec as P

MARGIN = 64
LANES = 128
SUBLANES = 8
STEP_SIZE = 0.25
MESH_ID = pl.DeviceIdType.MESH

DIRS = ((-1, 0), (1, 0), (0, -1), (0, 1), (-1, -1), (-1, 1), (1, -1), (1, 1))
OPP = tuple(DIRS.index((-a, -b)) for a, b in DIRS)


def dft_tables(length):
    k = np.arange(length)
    angle = 2.0 * np.pi * (np.outer(k, k) % length) / length
    c = np.cos(angle) / np.sqrt(length)
    s = np.sin(angle) / np.sqrt(length)
    plus = np.block([[c, s], [-s, c]])
    minus = np.block([[c, -s], [s, c]])

    def split(t):
        hi = t.astype(jnp.bfloat16)
        lo = (t - hi.astype(np.float64)).astype(jnp.bfloat16)
        return hi, lo

    ph, pw = split(plus)
    mh, mw = split(minus)
    right_f = np.concatenate([mh, mh, mw], axis=0)
    left_f = np.concatenate([ph, ph, pw], axis=1)
    left_b = np.concatenate([mh, mh, mw], axis=1)
    right_b = np.concatenate([ph, ph, pw], axis=0)
    return right_f, left_f, left_b, right_b


def neighbour_flags():
    row, col = lax.axis_index("row"), lax.axis_index("col")
    rows, cols = lax.axis_size("row"), lax.axis_size("col")
    flags = []
    for a, b in DIRS:
        r, c = row + a, col + b
        ok = jnp.logical_and(jnp.logical_and(r >= 0, r < rows), jnp.logical_and(c >= 0, c < cols))
        flags.append(ok)
    return flags


def target(step):
    return (lax.axis_index("row") + step[0], lax.axis_index("col") + step[1], lax.axis_index("mode"))


def enter(flags, others):
    barrier = pltpu.get_barrier_semaphore()
    total = jnp.int32(len(others))
    for flag, step in zip(flags, DIRS):
        total = total + flag.astype(jnp.int32)

        @pl.when(flag)
        def _():
            pl.semaphore_signal(barrier, inc=1, device_id=target(step), device_id_type=MESH_ID)

    for device in others:
        pl.semaphore_signal(barrier, inc=1, device_id=device, device_id_type=MESH_ID)
    pl.semaphore_wait(barrier, total)


def rim_copies(parts, slots, send, recv):
    return [
        pltpu.make_async_remote_copy(
            src_ref=parts[i], dst_ref=slots[i], send_sem=send.at[i], recv_sem=recv.at[i],
            device_id=target(DIRS[i]), device_id_type=MESH_ID,
        )
        for i in range(len(DIRS))
    ]


def gather_kernel(
    modes, cols, obj, pr, pi, halo_row, halo_col, halo_corner, others,
    send, recv, psend, precv, fsend, frecv,
):
    row, col, mode = lax.axis_index("row"), lax.axis_index("col"), lax.axis_index("mode")
    height, width = obj.shape[1], obj.shape[2]
    flags = neighbour_flags()
    parity = col % 2
    paired = cols % 2 == 0
    partner = col + 1 - 2 * parity
    peers = [(row, col, (mode + k) % modes) for k in range(1, modes)]
    enter(flags, peers)

    sides = (0, 1) if not paired else (None,)

    def probe_copy(k, side):
        source = (pr, pi)[side]
        return pltpu.make_async_remote_copy(
            src_ref=source.at[0], dst_ref=others.at[k, side], send_sem=psend.at[k, side],
            recv_sem=precv.at[k, side], device_id=peers[k], device_id_type=MESH_ID,
        )

    def forward_copy(k, side):
        return pltpu.make_async_remote_copy(
            src_ref=others.at[k, side], dst_ref=others.at[k, side], send_sem=fsend.at[k, side],
            recv_sem=frecv.at[k, side], device_id=(row, partner, mode), device_id_type=MESH_ID,
        )

    for k in reversed(range(modes - 1)):
        for side in (0, 1):
            if paired:
                @pl.when(parity == side)
                def _():
                    probe_copy(k, side).start()
            else:
                probe_copy(k, side).start()

    bands = [pl.ds(0, MARGIN), pl.ds(height - MARGIN, MARGIN)]
    strips = [pl.ds(0, LANES), pl.ds(width - LANES, LANES)]
    parts, slots = [], []
    for a, b in DIRS:
        rs = pl.ds(0, height) if a == 0 else bands[(a + 1) // 2]
        cs = pl.ds(0, width) if b == 0 else strips[(b + 1) // 2]
        parts.append(obj.at[:, rs, cs])
        ia, ib = (1 - a) // 2, (1 - b) // 2
        if b == 0:
            slots.append(halo_row.at[ia])
        elif a == 0:
            slots.append(halo_col.at[ib])
        else:
            slots.append(halo_corner.at[ia * 2 + ib])
    copies = rim_copies(parts, slots, send, recv)
    for i in range(len(DIRS)):
        @pl.when(flags[i])
        def _():
            copies[i].start()

    if paired:
        for k in range(modes - 1):
            for side in (0, 1):
                @pl.when(parity == side)
                def _():
                    probe_copy(k, side).wait_recv()
                    forward_copy(k, side).start()
        for k in range(modes - 1):
            for side in (0, 1):
                @pl.when(parity == side)
                def _():
                    probe_copy(k, side).wait_send()
                    forward_copy(k, side).wait_send()
                    forward_copy(k, 1 - side).wait_recv()
    else:
        for k in range(modes - 1):
            for side in (0, 1):
                probe_copy(k, side).wait()
    for i in range(len(DIRS)):
        @pl.when(flags[i])
        def _():
            copies[i].wait_send()

        @pl.when(flags[OPP[i]])
        def _():
            copies[i].wait_recv()


def gather(obj, pr, pi):
    modes, cols = lax.axis_size("mode"), lax.axis_size("col")
    _, height, width = obj.shape
    frame = pr.shape[-1]
    f32 = jnp.float32
    sem = pltpu.SemaphoreType.DMA
    return pl.pallas_call(
        functools.partial(gather_kernel, modes, cols),
        out_shape=[
            jax.ShapeDtypeStruct((2, 2, MARGIN, width), f32),
            jax.ShapeDtypeStruct((2, 2, height, LANES), f32),
            jax.ShapeDtypeStruct((4, 2, MARGIN, LANES), f32),
            jax.ShapeDtypeStruct((modes - 1, 2, frame, frame), f32),
        ],
        in_specs=[pl.BlockSpec(memory_space=pl.ANY)] * 3,
        out_specs=[pl.BlockSpec(memory_space=pl.ANY)] * 4,
        scratch_shapes=[
            sem((8,)), sem((8,)),
            sem((modes - 1, 2)), sem((modes - 1, 2)),
            sem((modes - 1, 2)), sem((modes - 1, 2)),
        ],
        compiler_params=pltpu.CompilerParams(collective_id=0, has_side_effects=True),
        name="gather",
    )(obj, pr, pi)


def split(x):
    hi = x.astype(jnp.bfloat16)
    lo = (x - hi.astype(jnp.float32)).astype(jnp.bfloat16)
    return hi, lo


def apply_right(x, table):
    hi, lo = split(x)
    return jnp.dot(
        jnp.concatenate([hi, lo, hi], axis=1), table, preferred_element_type=jnp.float32
    )


def apply_left(table, x):
    hi, lo = split(x)
    return jnp.dot(
        table, jnp.concatenate([hi, lo, hi], axis=0), preferred_element_type=jnp.float32
    )


def frames_kernel(
    modes, pos, cnt, obj, halo_row, halo_col, halo_corner, pr, pi, others, amp, rf, lf, lb, rb,
    acc, win, probe, tgt, sems, asems,
):
    height, width = obj.shape[1], obj.shape[2]
    frame = pr.shape[-1]
    rows, cols = win.shape[1], win.shape[2]
    slots = amp.shape[2]
    tall = frame + SUBLANES
    flags = neighbour_flags()
    center = (pl.ds(0, 2), pl.ds(MARGIN, height), pl.ds(LANES, width))

    loads = [
        (obj, win.at[center]),
        (obj, acc.at[center]),
        (pr.at[0], probe.at[0, 0]),
        (pi.at[0], probe.at[0, 1]),
    ]
    copies = [pltpu.make_async_copy(s, d, sems.at[i]) for i, (s, d) in enumerate(loads)]
    copies.append(
        pltpu.make_async_copy(others, probe.at[pl.ds(1, modes - 1)], sems.at[len(loads)])
    )
    for copy in copies:
        copy.start()
    targets = [pltpu.make_async_copy(amp.at[0, 0], tgt, asems.at[0])]
    for copy in targets:
        copy.start()

    acc[:, pl.ds(0, MARGIN), :] = jnp.zeros((2, MARGIN, cols), jnp.float32)
    acc[:, pl.ds(MARGIN + height, MARGIN), :] = jnp.zeros((2, MARGIN, cols), jnp.float32)
    acc[:, pl.ds(MARGIN, height), pl.ds(0, LANES)] = jnp.zeros((2, height, LANES), jnp.float32)
    acc[:, pl.ds(MARGIN, height), pl.ds(LANES + width, LANES)] = jnp.zeros(
        (2, height, LANES), jnp.float32
    )

    base = len(copies)
    for i, (a, b) in enumerate(DIRS):
        rs = (pl.ds(0, MARGIN), pl.ds(MARGIN, height), pl.ds(MARGIN + height, MARGIN))[a + 1]
        cs = (pl.ds(0, LANES), pl.ds(LANES, width), pl.ds(LANES + width, LANES))[b + 1]
        ia, ib = (a + 1) // 2, (b + 1) // 2
        if b == 0:
            source = halo_row.at[ia]
        elif a == 0:
            source = halo_col.at[ib]
        else:
            source = halo_corner.at[ia * 2 + ib]
        place = win.at[:, rs, cs]
        copy = pltpu.make_async_copy(source, place, sems.at[base + i])

        @pl.when(flags[i])
        def _():
            copy.start()

        @pl.when(jnp.logical_not(flags[i]))
        def _():
            place[...] = jnp.zeros(place.shape, jnp.float32)

        copies.append(copy)

    for copy in copies[:base]:
        copy.wait()
    for i in range(len(DIRS)):
        @pl.when(flags[i])
        def _():
            copies[base + i].wait()
    for copy in targets:
        copy.wait()

    def window_of(top, lift, first, shift):
        out = []
        for part in range(2):
            wide = win[part, pl.ds(top, tall), pl.ds(first, 2 * LANES)]
            wide = pltpu.roll(wide, shift, axis=1)[:, :frame]
            out.append(pltpu.roll(wide, (tall - lift) % tall, axis=0)[:frame])
        return out

    def place_of(slot):
        a = pos[0, 0, slot, 0]
        b = pos[0, 0, slot, 1] + (LANES - MARGIN)
        q = lax.div(b, LANES)
        top = lax.div(a, SUBLANES)
        lift = a - top * SUBLANES
        return pl.multiple_of(top * SUBLANES, SUBLANES), lift, pl.multiple_of(q * LANES, LANES), b - q * LANES

    def contribution(slot):
        top, lift, first, rest = place_of(slot)
        re, im = window_of(top, lift, first, (2 * LANES - rest) % (2 * LANES))
        waves = []
        for m in range(modes):
            p, q = probe[m, 0], probe[m, 1]
            waves.append(jnp.concatenate([p * re - q * im, p * im + q * re], axis=1))
        z = apply_right(jnp.concatenate(waves, axis=0), rf[...])
        z = jnp.concatenate(
            [
                jnp.concatenate([z[m * frame:(m + 1) * frame, :frame] for m in range(modes)], axis=1),
                jnp.concatenate([z[m * frame:(m + 1) * frame, frame:] for m in range(modes)], axis=1),
            ],
            axis=0,
        )
        y = apply_left(lf[...], z)
        power = y[:frame] * y[:frame] + y[frame:] * y[frame:]
        intensity = power[:, :frame]
        for m in range(1, modes):
            intensity = intensity + power[:, m * frame:(m + 1) * frame]
        keep = 1.0 - tgt[slot] / jnp.maximum(jnp.sqrt(intensity), 1.0)
        keep = jnp.concatenate([keep] * modes, axis=1)
        keep = jnp.concatenate([keep] * 2, axis=0)
        back = apply_left(lb[...], y * keep)
        back = jnp.concatenate(
            [
                jnp.concatenate(
                    [back[:frame, m * frame:(m + 1) * frame], back[frame:, m * frame:(m + 1) * frame]],
                    axis=1,
                )
                for m in range(modes)
            ],
            axis=0,
        )
        back = apply_right(back, rb[...])
        gr = jnp.zeros((frame, frame), jnp.float32)
        gi = jnp.zeros((frame, frame), jnp.float32)
        for m in range(modes):
            p, q = probe[m, 0], probe[m, 1]
            br = back[m * frame:(m + 1) * frame, :frame]
            bi = back[m * frame:(m + 1) * frame, frame:]
            gr = gr + (p * br + q * bi)
            gi = gi + (p * bi - q * br)
        return gr, gi

    def deposit(slot, gr, gi):
        top, lift, first, rest = place_of(slot)
        for part, g in enumerate((gr, gi)):
            wide = jnp.concatenate([g * -STEP_SIZE, jnp.zeros((SUBLANES, frame), jnp.float32)], axis=0)
            wide = pltpu.roll(wide, lift, axis=0)
            wide = jnp.concatenate([wide, jnp.zeros_like(wide)], axis=1)
            wide = pltpu.roll(wide, rest, axis=1)
            where = (part, pl.ds(top, tall), pl.ds(first, 2 * LANES))
            acc[where] = acc[where] + wide

    active = jnp.minimum(cnt[0, 0], slots)

    def pair(i, carry):
        s0 = 2 * i
        s1 = jnp.minimum(2 * i + 1, slots - 1)
        g0 = contribution(s0)
        g1 = contribution(s1)
        w = jnp.where(2 * i + 1 < active, 1.0, 0.0).astype(jnp.float32)
        deposit(s0, *g0)
        deposit(s1, g1[0] * w, g1[1] * w)
        return carry

    lax.fori_loop(0, (active + 1) // 2, pair, 0)


def frames(obj, halos, pr, pi, others, amp, pos, cnt):
    modes = lax.axis_size("mode")
    _, height, width = obj.shape
    frame = pr.shape[-1]
    slots = amp.shape[2]
    f32 = jnp.float32
    rows, cols = height + 2 * MARGIN + SUBLANES, width + 2 * LANES
    tables = [jnp.asarray(t) for t in dft_tables(frame)]
    smem = pl.BlockSpec(memory_space=pltpu.SMEM)
    anym = pl.BlockSpec(memory_space=pl.ANY)
    vmem = pl.BlockSpec(memory_space=pltpu.VMEM)
    return pl.pallas_call(
        functools.partial(frames_kernel, modes),
        out_shape=jax.ShapeDtypeStruct((2, rows, cols), f32),
        in_specs=[smem, smem] + [anym] * 8 + [vmem] * 4,
        out_specs=vmem,
        scratch_shapes=[
            pltpu.VMEM((2, rows, cols), f32),
            pltpu.VMEM((modes, 2, frame, frame), f32),
            pltpu.VMEM((slots, frame, frame), f32),
            pltpu.SemaphoreType.DMA((16,)),
            pltpu.SemaphoreType.DMA((1,)),
        ],
        name="frames",
    )(pos, cnt, obj, *halos, pr, pi, others, amp, *tables)


def fold_kernel(grad, out, got_row, got_col, got_corner, send, recv, own):
    height, width = out.shape[1], out.shape[2]
    flags = neighbour_flags()
    mine = pltpu.make_async_copy(
        grad.at[:, pl.ds(MARGIN, height), pl.ds(LANES, width)], out, own.at[0]
    )
    mine.start()
    enter(flags, [])
    parts, slots = [], []
    for a, b in DIRS:
        rs = (pl.ds(0, MARGIN), pl.ds(MARGIN, height), pl.ds(MARGIN + height, MARGIN))[a + 1]
        cs = (pl.ds(0, LANES), pl.ds(LANES, width), pl.ds(LANES + width, LANES))[b + 1]
        parts.append(grad.at[:, rs, cs])
        ia, ib = (1 - a) // 2, (1 - b) // 2
        if b == 0:
            slots.append(got_row.at[ia])
        elif a == 0:
            slots.append(got_col.at[ib])
        else:
            slots.append(got_corner.at[ia * 2 + ib])
    copies = rim_copies(parts, slots, send, recv)
    for i in range(len(DIRS)):
        @pl.when(flags[i])
        def _():
            copies[i].start()
    mine.wait()
    half = LANES - MARGIN
    for i, (a, b) in enumerate(DIRS):
        @pl.when(flags[OPP[i]])
        def _():
            copies[i].wait_recv()
            ia, ib = (1 - a) // 2, (1 - b) // 2
            r0 = (0, height - MARGIN)[ia] if a else 0
            if b == 0:
                out[:, pl.ds(r0, MARGIN), :] = out[:, pl.ds(r0, MARGIN), :] + got_row[ia]
            else:
                c0 = (0, width - LANES)[ib]
                n = MARGIN if a else height
                value = got_corner[ia * 2 + ib] if a else got_col[ib]
                out[:, pl.ds(r0, n), pl.ds(c0, LANES)] = out[:, pl.ds(r0, n), pl.ds(c0, LANES)] + value

    for i in range(len(DIRS)):
        @pl.when(flags[i])
        def _():
            copies[i].wait_send()


def fold(grad, height, width):
    f32 = jnp.float32
    sem = pltpu.SemaphoreType.DMA
    return pl.pallas_call(
        fold_kernel,
        out_shape=jax.ShapeDtypeStruct((2, height, width), f32),
        in_specs=[pl.BlockSpec(memory_space=pl.ANY)],
        out_specs=pl.BlockSpec(memory_space=pltpu.VMEM),
        scratch_shapes=[
            pltpu.VMEM((2, 2, MARGIN, width), f32),
            pltpu.VMEM((2, 2, height, LANES), f32),
            pltpu.VMEM((4, 2, MARGIN, LANES), f32),
            sem((8,)), sem((8,)), sem((1,)),
        ],
        compiler_params=pltpu.CompilerParams(collective_id=1, has_side_effects=True),
        name="fold",
    )(grad)


def per_device(object_field, probe_real, probe_imag, amplitude, positions, counts):
    *halos, others = gather(object_field, probe_real, probe_imag)
    grad = frames(object_field, halos, probe_real, probe_imag, others, amplitude, positions, counts)
    return fold(grad, object_field.shape[1], object_field.shape[2])


def solution(mesh):
    in_specs = (
        P(None, "row", "col"),
        P("mode", None, None),
        P("mode", None, None),
        P("row", "col", None, None, None),
        P("row", "col", None, None),
        P("row", "col"),
    )
    out_specs = P(None, "row", "col")
    return jax.shard_map(
        per_device, mesh=mesh, in_specs=in_specs, out_specs=out_specs, check_vma=False
    )
```

```python
import functools

import jax
import jax.numpy as jnp
import numpy as np
from jax import lax
from jax.experimental import pallas as pl
from jax.experimental.pallas import tpu as pltpu
from jax.sharding import PartitionSpec as P

MARGIN = 64
LANES = 128
SUBLANES = 8
STEP_SIZE = 0.25
MESH_ID = pl.DeviceIdType.MESH

DIRS = ((-1, 0), (1, 0), (0, -1), (0, 1), (-1, -1), (-1, 1), (1, -1), (1, 1))
OPP = tuple(DIRS.index((-a, -b)) for a, b in DIRS)


def dft_tables(length):
    k = np.arange(length)
    angle = 2.0 * np.pi * (np.outer(k, k) % length) / length
    c = np.cos(angle) / np.sqrt(length)
    s = np.sin(angle) / np.sqrt(length)
    plus = np.block([[c, s], [-s, c]])
    minus = np.block([[c, -s], [s, c]])

    def split(t):
        hi = t.astype(jnp.bfloat16)
        lo = (t - hi.astype(np.float64)).astype(jnp.bfloat16)
        return hi, lo

    ph, pw = split(plus)
    mh, mw = split(minus)
    right_f = np.concatenate([mh, mh, mw], axis=0)
    left_f = np.concatenate([ph, ph, pw], axis=1)
    left_b = np.concatenate([mh, mh, mw], axis=1)
    right_b = np.concatenate([ph, ph, pw], axis=0)
    return right_f, left_f, left_b, right_b


def neighbour_flags():
    row, col = lax.axis_index("row"), lax.axis_index("col")
    rows, cols = lax.axis_size("row"), lax.axis_size("col")
    flags = []
    for a, b in DIRS:
        r, c = row + a, col + b
        ok = jnp.logical_and(jnp.logical_and(r >= 0, r < rows), jnp.logical_and(c >= 0, c < cols))
        flags.append(ok)
    return flags


def target(step):
    return (lax.axis_index("row") + step[0], lax.axis_index("col") + step[1], lax.axis_index("mode"))


def enter(flags, others):
    barrier = pltpu.get_barrier_semaphore()
    total = jnp.int32(len(others))
    for flag, step in zip(flags, DIRS):
        total = total + flag.astype(jnp.int32)

        @pl.when(flag)
        def _():
            pl.semaphore_signal(barrier, inc=1, device_id=target(step), device_id_type=MESH_ID)

    for device in others:
        pl.semaphore_signal(barrier, inc=1, device_id=device, device_id_type=MESH_ID)
    pl.semaphore_wait(barrier, total)


def rim_copies(parts, slots, send, recv):
    return [
        pltpu.make_async_remote_copy(
            src_ref=parts[i], dst_ref=slots[i], send_sem=send.at[i], recv_sem=recv.at[i],
            device_id=target(DIRS[i]), device_id_type=MESH_ID,
        )
        for i in range(len(DIRS))
    ]


def split(x):
    hi = x.astype(jnp.bfloat16)
    lo = (x - hi.astype(jnp.float32)).astype(jnp.bfloat16)
    return hi, lo


def apply_right(x, table):
    hi, lo = split(x)
    return jnp.dot(
        jnp.concatenate([hi, lo, hi], axis=1), table, preferred_element_type=jnp.float32
    )


def apply_left(table, x):
    hi, lo = split(x)
    return jnp.dot(
        table, jnp.concatenate([hi, lo, hi], axis=0), preferred_element_type=jnp.float32
    )


def step_kernel(
    modes, cols, pos, cnt, obj, pr, pi, amp, rf_in, lf_in, lb_in, rb_in,
    out,
    win, probe, tgt, patch, spec, padded, got_row, got_strip, got_corner, rim_row, strip,
    rf, lf, lb, rb,
    send, recv, csend, crecv, psend, precv, fsend, frecv, rsend, rrecv, local,
):
    row, col, mode = lax.axis_index("row"), lax.axis_index("col"), lax.axis_index("mode")
    height, width = obj.shape[1], obj.shape[2]
    frame = pr.shape[-1]
    slots = amp.shape[2]
    tall = frame + SUBLANES
    flags = neighbour_flags()
    parity = col % 2
    paired = cols % 2 == 0
    partner = col + 1 - 2 * parity
    peers = [(row, col, (mode + k) % modes) for k in range(1, modes)]
    f32 = jnp.float32

    bands = (pl.ds(0, MARGIN), pl.ds(MARGIN, height), pl.ds(MARGIN + height, MARGIN))
    strips = (pl.ds(0, LANES), pl.ds(LANES, width), pl.ds(LANES + width, LANES))

    loads = [
        (obj, win.at[:, bands[1], strips[1]]),
        (pr.at[0], probe.at[0, 0]),
        (pi.at[0], probe.at[0, 1]),
        (amp.at[0, 0], tgt),
        (rf_in, rf), (lf_in, lf), (lb_in, lb), (rb_in, rb),
    ]
    loads = [pltpu.make_async_copy(a, b, local.at[i]) for i, (a, b) in enumerate(loads)]
    for copy in loads:
        copy.start()

    enter(flags, peers)

    def probe_copy(k, side):
        return pltpu.make_async_remote_copy(
            src_ref=(pr, pi)[side].at[0], dst_ref=probe.at[k, side], send_sem=psend.at[k - 1, side],
            recv_sem=precv.at[k - 1, side], device_id=peers[k - 1], device_id_type=MESH_ID,
        )

    def forward_copy(k, side):
        return pltpu.make_async_remote_copy(
            src_ref=probe.at[k, side], dst_ref=probe.at[k, side], send_sem=fsend.at[k - 1, side],
            recv_sem=frecv.at[k - 1, side], device_id=(row, partner, mode), device_id_type=MESH_ID,
        )

    def sided(action):
        for side in (0, 1):
            if paired:
                @pl.when(parity == side)
                def _():
                    action(side)
            else:
                action(side)

    for k in range(1, modes):
        sided(lambda side: probe_copy(k, side).start())

    def side_copy(i):
        a, b = DIRS[i]
        rs = {-1: pl.ds(0, MARGIN), 0: pl.ds(0, height), 1: pl.ds(height - MARGIN, MARGIN)}[a]
        cs = {-1: pl.ds(0, LANES), 0: pl.ds(0, width), 1: pl.ds(width - LANES, LANES)}[b]
        return pltpu.make_async_remote_copy(
            src_ref=obj.at[:, rs, cs], dst_ref=win.at[:, bands[1 - a], strips[1 - b]],
            send_sem=send.at[i], recv_sem=recv.at[i], device_id=target(DIRS[i]), device_id_type=MESH_ID,
        )

    def corner_copy(i, up):
        b = DIRS[i][1]
        cs = {-1: pl.ds(LANES, LANES), 1: pl.ds(width, LANES)}[b]
        rs = bands[up + 1]
        j = (i - 2) * 2 + (up + 1) // 2
        return pltpu.make_async_remote_copy(
            src_ref=win.at[:, rs, cs], dst_ref=win.at[:, rs, strips[1 - b]],
            send_sem=csend.at[j], recv_sem=crecv.at[j], device_id=target(DIRS[i]), device_id_type=MESH_ID,
        )

    for i in range(4):
        @pl.when(flags[i])
        def _():
            side_copy(i).start()

    for i, (a, b) in enumerate(DIRS):
        @pl.when(jnp.logical_not(flags[i]))
        def _():
            place = win.at[:, bands[a + 1], strips[b + 1]]
            place[...] = jnp.zeros(place.shape, f32)

    win[:, pl.ds(2 * MARGIN + height, SUBLANES), :] = jnp.zeros((2, SUBLANES, width + 2 * LANES), f32)

    def clear(s, carry):
        padded[s] = jnp.zeros(padded.shape[1:], f32)
        return carry

    lax.fori_loop(0, slots, clear, 0)

    for copy in loads:
        copy.wait()

    for i in (0, 1):
        up = DIRS[OPP[i]][0]

        @pl.when(flags[OPP[i]])
        def _():
            side_copy(i).wait_recv()

        for j in (2, 3):
            @pl.when(jnp.logical_and(flags[OPP[i]], flags[j]))
            def _():
                corner_copy(j, up).start()

    if paired:
        for k in range(1, modes):
            def relay(side):
                probe_copy(k, side).wait_recv()
                forward_copy(k, side).start()

            sided(relay)

    for i in (2, 3):
        @pl.when(flags[OPP[i]])
        def _():
            side_copy(i).wait_recv()

        for up, r in ((-1, 0), (1, 1)):
            @pl.when(jnp.logical_and(flags[OPP[i]], flags[r]))
            def _():
                corner_copy(i, up).wait_recv()

    def place_of(slot):
        a = pos[0, 0, 0, slot]
        b = pos[0, 0, 1, slot] + (LANES - MARGIN)
        q = lax.div(b, LANES)
        top = lax.div(a, SUBLANES)
        return top, a - top * SUBLANES, q, b - q * LANES

    def cut(slot, carry):
        top, lift, q, rest = place_of(slot)
        shift = (2 * LANES - rest) % (2 * LANES)
        for part in range(2):
            wide = win[part, pl.ds(top * SUBLANES, tall), pl.ds(q * LANES, 2 * LANES)]
            wide = pltpu.roll(wide, shift, axis=1)[:, :frame]
            patch[slot, part] = pltpu.roll(wide, (tall - lift) % tall, axis=0)[:frame]
        return carry

    lax.fori_loop(0, slots, cut, 0)

    group = min(slots, 4)

    def forward(k):
        def some(g, carry):
            p, q = probe[k, 0], probe[k, 1]
            waves = []
            for j in range(group):
                re, im = patch[g * group + j, 0], patch[g * group + j, 1]
                waves.append(jnp.concatenate([p * re - q * im, p * im + q * re], axis=1))
            z = apply_right(jnp.concatenate(waves, axis=0), rf[...])
            z = jnp.concatenate(
                [
                    jnp.concatenate([z[j * frame:(j + 1) * frame, :frame] for j in range(group)], axis=1),
                    jnp.concatenate([z[j * frame:(j + 1) * frame, frame:] for j in range(group)], axis=1),
                ],
                axis=0,
            )
            y = apply_left(lf[...], z)
            for j in range(group):
                spec[k, g * group + j] = y[:, j * frame:(j + 1) * frame]
            return carry

        lax.fori_loop(0, slots // group, some, 0)

    for k in range(modes):
        if k:
            if paired:
                sided(lambda side: forward_copy(k, 1 - side).wait_recv())
            else:
                sided(lambda side: probe_copy(k, side).wait_recv())
        forward(k)

    def contribution(slot):
        y = jnp.concatenate([spec[m, slot] for m in range(modes)], axis=1)
        power = y[:frame] * y[:frame] + y[frame:] * y[frame:]
        intensity = power[:, :frame]
        for m in range(1, modes):
            intensity = intensity + power[:, m * frame:(m + 1) * frame]
        keep = 1.0 - tgt[slot] / jnp.maximum(jnp.sqrt(intensity), 1.0)
        keep = jnp.concatenate([keep] * modes, axis=1)
        keep = jnp.concatenate([keep] * 2, axis=0)
        back = apply_left(lb[...], y * keep)
        back = jnp.concatenate(
            [
                jnp.concatenate(
                    [back[:frame, m * frame:(m + 1) * frame], back[frame:, m * frame:(m + 1) * frame]],
                    axis=1,
                )
                for m in range(modes)
            ],
            axis=0,
        )
        back = apply_right(back, rb[...])
        gr = jnp.zeros((frame, frame), f32)
        gi = jnp.zeros((frame, frame), f32)
        for m in range(modes):
            p, q = probe[m, 0], probe[m, 1]
            br = back[m * frame:(m + 1) * frame, :frame]
            bi = back[m * frame:(m + 1) * frame, frame:]
            gr = gr + (p * br + q * bi)
            gi = gi + (p * bi - q * br)
        return gr, gi

    def keep_padded(slot, gr, gi):
        _, lift, _, rest = place_of(slot)
        weight = jnp.where(slot < cnt[0, 0], -STEP_SIZE, 0.0).astype(f32)
        for part, g in enumerate((gr, gi)):
            wide = jnp.concatenate([g * weight, jnp.zeros((SUBLANES, frame), f32)], axis=0)
            wide = pltpu.roll(wide, lift, axis=0)
            wide = jnp.concatenate([wide, jnp.zeros_like(wide)], axis=1)
            padded[slot, part, pl.ds(tall, tall), pl.ds(LANES, 2 * LANES)] = pltpu.roll(wide, rest, axis=1)

    def pair(i, carry):
        g0 = contribution(2 * i)
        g1 = contribution(2 * i + 1)
        keep_padded(2 * i, *g0)
        keep_padded(2 * i + 1, *g1)
        return carry

    lax.fori_loop(0, slots // 2, pair, 0)

    for j in (2, 3):
        for up, r in ((-1, 0), (1, 1)):
            @pl.when(jnp.logical_and(flags[r], flags[j]))
            def _():
                corner_copy(j, up).wait_send()

    places = [place_of(s) for s in range(slots)]

    def block_sum(part, j, t, total):
        for s in range(slots):
            top, _, q, _ = places[s]
            start = jnp.clip(tall // SUBLANES + j * (frame // SUBLANES) - top, 0, 2 * tall // SUBLANES) * SUBLANES
            lane = jnp.clip(t - q + 1, 0, 3) * LANES
            piece = padded[
                s, part, pl.ds(start, frame),
                pl.ds(lane, LANES),
            ]
            total = piece if total is None else total + piece
        return total

    n_lane = width // LANES + 2

    def rows_of(j, carry):
        r = pl.multiple_of(j * frame, frame)
        for part in range(2):
            for t in range(n_lane):
                where = (part, pl.ds(r, frame), pl.ds(t * LANES, LANES))
                edge = t in (0, n_lane - 1)
                win[where] = block_sum(part, j, t, None if edge else jnp.where(inner(j), win[where], 0.0))
        return carry

    lane_id = lax.broadcasted_iota(jnp.int32, (frame, LANES), 1)
    row_id = lax.broadcasted_iota(jnp.int32, (frame, LANES), 0)

    def inner(j):
        r = row_id + j * frame
        return jnp.logical_and(r >= MARGIN, r < MARGIN + height)

    lax.fori_loop(0, (height + 2 * MARGIN) // frame, rows_of, 0)

    for i in range(2):
        rim_row[i] = win[:, bands[2 * i], strips[1]]
    low = lax.broadcasted_iota(jnp.int32, (height + 2 * MARGIN, LANES), 1) < MARGIN
    every = pl.ds(0, height + 2 * MARGIN)
    re, im = win[0, every, strips[0]], win[1, every, strips[0]]
    strip[0] = jnp.where(low, pltpu.roll(re, MARGIN, axis=1), im)
    re, im = win[0, every, strips[2]], win[1, every, strips[2]]
    strip[1] = jnp.where(low, re, pltpu.roll(im, MARGIN, axis=1))

    parts, places_to = [], []
    for a, b in DIRS:
        if b == 0:
            parts.append(rim_row.at[(a + 1) // 2])
            places_to.append(got_row.at[(a + 1) // 2])
        elif a == 0:
            parts.append(strip.at[(b + 1) // 2, bands[1]])
            places_to.append(got_strip.at[(b + 1) // 2])
        else:
            parts.append(strip.at[(b + 1) // 2, bands[a + 1]])
            places_to.append(got_corner.at[(a + 1) + (b + 1) // 2])
    rims = rim_copies(parts, places_to, rsend, rrecv)
    for i in range(len(DIRS)):
        @pl.when(flags[i])
        def _():
            rims[i].start()

    out[...] = win[:, bands[1], strips[1]]

    def add_packed(value, b, r0, n):
        turned = pltpu.roll(value, MARGIN, axis=1)
        first = lax.broadcasted_iota(jnp.int32, (n, LANES), 1) < MARGIN
        if b < 0:
            c0, re, im, here = width - LANES, turned, value, jnp.logical_not(first)
        else:
            c0, re, im, here = 0, value, turned, first
        for part, v in enumerate((re, im)):
            where = (part, pl.ds(r0, n), pl.ds(c0, LANES))
            out[where] = out[where] + jnp.where(here, v, 0.0)

    for i, (a, b) in enumerate(DIRS):
        @pl.when(flags[OPP[i]])
        def _():
            rims[i].wait_recv()
            r0 = {-1: height - MARGIN, 0: 0, 1: 0}[a]
            if b == 0:
                where = (pl.ds(0, 2), pl.ds(r0, MARGIN), pl.ds(0, width))
                out[where] = out[where] + got_row[(a + 1) // 2]
            elif a == 0:
                add_packed(got_strip[(b + 1) // 2], b, 0, height)
            else:
                add_packed(got_corner[(a + 1) + (b + 1) // 2], b, r0, MARGIN)

    for k in range(1, modes):
        def sent(side):
            probe_copy(k, side).wait_send()
            if paired:
                forward_copy(k, side).wait_send()

        sided(sent)
    for i in range(4):
        @pl.when(flags[i])
        def _():
            side_copy(i).wait_send()
    for i in range(len(DIRS)):
        @pl.when(flags[i])
        def _():
            rims[i].wait_send()


def per_device(object_field, probe_real, probe_imag, amplitude, positions, counts):
    modes, cols = lax.axis_size("mode"), lax.axis_size("col")
    _, height, width = object_field.shape
    frame = probe_real.shape[-1]
    slots = amplitude.shape[2]
    f32 = jnp.float32
    tall = frame + SUBLANES
    tables = [jnp.asarray(t) for t in dft_tables(frame)]
    smem = pl.BlockSpec(memory_space=pltpu.SMEM)
    anym = pl.BlockSpec(memory_space=pl.ANY)
    sem = pltpu.SemaphoreType.DMA
    vmem = pltpu.VMEM
    return pl.pallas_call(
        functools.partial(step_kernel, modes, cols),
        out_shape=jax.ShapeDtypeStruct((2, height, width), f32),
        in_specs=[smem, smem] + [anym] * 8,
        out_specs=pl.BlockSpec(memory_space=vmem),
        scratch_shapes=[
            vmem((2, height + 2 * MARGIN + SUBLANES, width + 2 * LANES), f32),
            vmem((modes, 2, frame, frame), f32),
            vmem((slots, frame, frame), f32),
            vmem((slots, 2, frame, frame), f32),
            vmem((modes, slots, 2 * frame, frame), f32),
            vmem((slots, 2, 2 * tall + frame, 4 * LANES), f32),
            vmem((2, 2, MARGIN, width), f32),
            vmem((2, height, LANES), f32),
            vmem((4, MARGIN, LANES), f32),
            vmem((2, 2, MARGIN, width), f32),
            vmem((2, height + 2 * MARGIN, LANES), f32),
            *[vmem(t.shape, t.dtype) for t in tables],
            sem((4,)), sem((4,)),
            sem((4,)), sem((4,)),
            sem((modes - 1, 2)), sem((modes - 1, 2)),
            sem((modes - 1, 2)), sem((modes - 1, 2)),
            sem((8,)), sem((8,)),
            sem((8,)),
        ],
        compiler_params=pltpu.CompilerParams(collective_id=0, has_side_effects=True),
        name="gradient_step",
    )(jnp.swapaxes(positions, 2, 3), counts, object_field, probe_real, probe_imag, amplitude, *tables)


def solution(mesh):
    in_specs = (
        P(None, "row", "col"),
        P("mode", None, None),
        P("mode", None, None),
        P("row", "col", None, None, None),
        P("row", "col", None, None),
        P("row", "col"),
    )
    out_specs = P(None, "row", "col")
    return jax.shard_map(
        per_device, mesh=mesh, in_specs=in_specs, out_specs=out_specs, check_vma=False
    )
```

```python
import functools

import jax
import jax.numpy as jnp
import numpy as np
from jax import lax
from jax.experimental import pallas as pl
from jax.experimental.pallas import tpu as pltpu
from jax.sharding import PartitionSpec as P

MARGIN = 64
LANES = 128
SUBLANES = 8
STEP_SIZE = 0.25
MESH_ID = pl.DeviceIdType.MESH

DIRS = ((-1, 0), (1, 0), (0, -1), (0, 1), (-1, -1), (-1, 1), (1, -1), (1, 1))
OPP = tuple(DIRS.index((-a, -b)) for a, b in DIRS)


def dft_tables(length):
    k = np.arange(length)
    angle = 2.0 * np.pi * (np.outer(k, k) % length) / length
    c = np.cos(angle) / np.sqrt(length)
    s = np.sin(angle) / np.sqrt(length)
    plus = np.block([[c, s], [-s, c]])
    minus = np.block([[c, -s], [s, c]])

    def split(t):
        hi = t.astype(jnp.bfloat16)
        lo = (t - hi.astype(np.float64)).astype(jnp.bfloat16)
        return hi, lo

    ph, pw = split(plus)
    mh, mw = split(minus)
    right_f = np.concatenate([mh, mh, mw], axis=0)
    left_f = np.concatenate([ph, ph, pw], axis=1)
    left_b = np.concatenate([mh, mh, mw], axis=1)
    right_b = np.concatenate([ph, ph, pw], axis=0)
    return right_f, left_f, left_b, right_b


def neighbour_flags():
    row, col = lax.axis_index("row"), lax.axis_index("col")
    rows, cols = lax.axis_size("row"), lax.axis_size("col")
    flags = []
    for a, b in DIRS:
        r, c = row + a, col + b
        ok = jnp.logical_and(jnp.logical_and(r >= 0, r < rows), jnp.logical_and(c >= 0, c < cols))
        flags.append(ok)
    return flags


def target(step):
    return (lax.axis_index("row") + step[0], lax.axis_index("col") + step[1], lax.axis_index("mode"))


def enter(flags, others):
    barrier = pltpu.get_barrier_semaphore()
    total = jnp.int32(len(others))
    for flag, step in zip(flags, DIRS):
        total = total + flag.astype(jnp.int32)

        @pl.when(flag)
        def _():
            pl.semaphore_signal(barrier, inc=1, device_id=target(step), device_id_type=MESH_ID)

    for device in others:
        pl.semaphore_signal(barrier, inc=1, device_id=device, device_id_type=MESH_ID)
    pl.semaphore_wait(barrier, total)


def rim_copies(parts, slots, send, recv):
    return [
        pltpu.make_async_remote_copy(
            src_ref=parts[i], dst_ref=slots[i], send_sem=send.at[i], recv_sem=recv.at[i],
            device_id=target(DIRS[i]), device_id_type=MESH_ID,
        )
        for i in range(len(DIRS))
    ]


def split(x):
    hi = x.astype(jnp.bfloat16)
    lo = (x - hi.astype(jnp.float32)).astype(jnp.bfloat16)
    return hi, lo


def apply_right(x, table):
    hi, lo = split(x)
    return jnp.dot(
        jnp.concatenate([hi, lo, hi], axis=1), table, preferred_element_type=jnp.float32
    )


def apply_left(table, x):
    hi, lo = split(x)
    return jnp.dot(
        table, jnp.concatenate([hi, lo, hi], axis=0), preferred_element_type=jnp.float32
    )


def step_kernel(
    modes, cols, pos, cnt, obj, pr, pi, amp, rf_in, lf_in, lb_in, rb_in,
    out,
    win, probe, tgt, patch, spec, padded, got_row, got_strip, got_corner, rim_row, strip,
    rf, lf, lb, rb,
    send, recv, csend, crecv, psend, precv, fsend, frecv, rsend, rrecv, local,
):
    row, col, mode = lax.axis_index("row"), lax.axis_index("col"), lax.axis_index("mode")
    height, width = obj.shape[1], obj.shape[2]
    frame = pr.shape[-1]
    slots = amp.shape[2]
    tall = frame + SUBLANES
    flags = neighbour_flags()
    parity = col % 2
    paired = cols % 2 == 0
    partner = col + 1 - 2 * parity
    peers = [(row, col, (mode + k) % modes) for k in range(1, modes)]
    f32 = jnp.float32

    bands = (pl.ds(0, MARGIN), pl.ds(MARGIN, height), pl.ds(MARGIN + height, MARGIN))
    strips = (pl.ds(0, LANES), pl.ds(LANES, width), pl.ds(LANES + width, LANES))

    loads = [
        (obj, win.at[:, bands[1], strips[1]]),
        (pr.at[0], probe.at[0, 0]),
        (pi.at[0], probe.at[0, 1]),
        (amp.at[0, 0], tgt),
        (rf_in, rf), (lf_in, lf), (lb_in, lb), (rb_in, rb),
    ]
    loads = [pltpu.make_async_copy(a, b, local.at[i]) for i, (a, b) in enumerate(loads)]
    for copy in loads:
        copy.start()

    enter(flags, peers)

    def probe_copy(k, side):
        return pltpu.make_async_remote_copy(
            src_ref=(pr, pi)[side].at[0], dst_ref=probe.at[k, side], send_sem=psend.at[k - 1, side],
            recv_sem=precv.at[k - 1, side], device_id=peers[k - 1], device_id_type=MESH_ID,
        )

    def forward_copy(k, side):
        return pltpu.make_async_remote_copy(
            src_ref=probe.at[k, side], dst_ref=probe.at[k, side], send_sem=fsend.at[k - 1, side],
            recv_sem=frecv.at[k - 1, side], device_id=(row, partner, mode), device_id_type=MESH_ID,
        )

    def sided(action):
        for side in (0, 1):
            if paired:
                @pl.when(parity == side)
                def _():
                    action(side)
            else:
                action(side)

    for k in range(1, modes):
        sided(lambda side: probe_copy(k, side).start())

    def side_copy(i):
        a, b = DIRS[i]
        rs = {-1: pl.ds(0, MARGIN), 0: pl.ds(0, height), 1: pl.ds(height - MARGIN, MARGIN)}[a]
        cs = {-1: pl.ds(0, LANES), 0: pl.ds(0, width), 1: pl.ds(width - LANES, LANES)}[b]
        return pltpu.make_async_remote_copy(
            src_ref=obj.at[:, rs, cs], dst_ref=win.at[:, bands[1 - a], strips[1 - b]],
            send_sem=send.at[i], recv_sem=recv.at[i], device_id=target(DIRS[i]), device_id_type=MESH_ID,
        )

    def corner_copy(i, up):
        b = DIRS[i][1]
        cs = {-1: pl.ds(LANES, LANES), 1: pl.ds(width, LANES)}[b]
        rs = bands[up + 1]
        j = (i - 2) * 2 + (up + 1) // 2
        return pltpu.make_async_remote_copy(
            src_ref=win.at[:, rs, cs], dst_ref=win.at[:, rs, strips[1 - b]],
            send_sem=csend.at[j], recv_sem=crecv.at[j], device_id=target(DIRS[i]), device_id_type=MESH_ID,
        )

    for i in range(4):
        @pl.when(flags[i])
        def _():
            side_copy(i).start()

    for i, (a, b) in enumerate(DIRS):
        @pl.when(jnp.logical_not(flags[i]))
        def _():
            place = win.at[:, bands[a + 1], strips[b + 1]]
            place[...] = jnp.zeros(place.shape, f32)

    win[:, pl.ds(2 * MARGIN + height, SUBLANES), :] = jnp.zeros((2, SUBLANES, width + 2 * LANES), f32)

    def clear(s, carry):
        padded[s] = jnp.zeros(padded.shape[1:], f32)
        return carry

    lax.fori_loop(0, slots, clear, 0)

    for copy in loads:
        copy.wait()

    for i in (0, 1):
        up = DIRS[OPP[i]][0]

        @pl.when(flags[OPP[i]])
        def _():
            side_copy(i).wait_recv()

        for j in (2, 3):
            @pl.when(jnp.logical_and(flags[OPP[i]], flags[j]))
            def _():
                corner_copy(j, up).start()

    if paired:
        for k in range(1, modes):
            def relay(side):
                probe_copy(k, side).wait_recv()
                forward_copy(k, side).start()

            sided(relay)

    for i in (2, 3):
        @pl.when(flags[OPP[i]])
        def _():
            side_copy(i).wait_recv()

        for up, r in ((-1, 0), (1, 1)):
            @pl.when(jnp.logical_and(flags[OPP[i]], flags[r]))
            def _():
                corner_copy(i, up).wait_recv()

    def place_of(slot):
        a = pos[0, 0, 0, slot]
        b = pos[0, 0, 1, slot] + (LANES - MARGIN)
        q = lax.div(b, LANES)
        top = lax.div(a, SUBLANES)
        return top, a - top * SUBLANES, q, b - q * LANES

    def cut(slot, carry):
        top, lift, q, rest = place_of(slot)
        shift = (2 * LANES - rest) % (2 * LANES)
        for part in range(2):
            wide = win[part, pl.ds(top * SUBLANES, tall), pl.ds(q * LANES, 2 * LANES)]
            wide = pltpu.roll(wide, shift, axis=1)[:, :frame]
            patch[slot, part] = pltpu.roll(wide, (tall - lift) % tall, axis=0)[:frame]
        return carry

    lax.fori_loop(0, slots, cut, 0)

    group = min(slots, 4)

    def forward(k):
        p, q = probe[k, 0], probe[k, 1]
        groups = []
        for g in range(0, slots, group):
            waves = []
            for j in range(g, g + group):
                re, im = patch[j, 0], patch[j, 1]
                waves.append(jnp.concatenate([p * re - q * im, p * im + q * re], axis=1))
            groups.append(apply_right(jnp.concatenate(waves, axis=0), rf[...]))
        for g, z in zip(range(0, slots, group), groups):
            z = jnp.concatenate(
                [
                    jnp.concatenate([z[j * frame:(j + 1) * frame, :frame] for j in range(group)], axis=1),
                    jnp.concatenate([z[j * frame:(j + 1) * frame, frame:] for j in range(group)], axis=1),
                ],
                axis=0,
            )
            y = apply_left(lf[...], z)
            for j in range(group):
                spec[k, g + j] = y[:, j * frame:(j + 1) * frame]

    for k in range(modes):
        if k:
            if paired:
                sided(lambda side: forward_copy(k, 1 - side).wait_recv())
            else:
                sided(lambda side: probe_copy(k, side).wait_recv())
        forward(k)

    def contribution(slot):
        y = jnp.concatenate([spec[m, slot] for m in range(modes)], axis=1)
        power = y[:frame] * y[:frame] + y[frame:] * y[frame:]
        intensity = power[:, :frame]
        for m in range(1, modes):
            intensity = intensity + power[:, m * frame:(m + 1) * frame]
        keep = 1.0 - tgt[slot] / jnp.maximum(jnp.sqrt(intensity), 1.0)
        keep = jnp.concatenate([keep] * modes, axis=1)
        keep = jnp.concatenate([keep] * 2, axis=0)
        back = apply_left(lb[...], y * keep)
        back = jnp.concatenate(
            [
                jnp.concatenate(
                    [back[:frame, m * frame:(m + 1) * frame], back[frame:, m * frame:(m + 1) * frame]],
                    axis=1,
                )
                for m in range(modes)
            ],
            axis=0,
        )
        back = apply_right(back, rb[...])
        gr = jnp.zeros((frame, frame), f32)
        gi = jnp.zeros((frame, frame), f32)
        for m in range(modes):
            p, q = probe[m, 0], probe[m, 1]
            br = back[m * frame:(m + 1) * frame, :frame]
            bi = back[m * frame:(m + 1) * frame, frame:]
            gr = gr + (p * br + q * bi)
            gi = gi + (p * bi - q * br)
        return gr, gi

    def keep_padded(slot, gr, gi):
        _, lift, _, rest = place_of(slot)
        weight = jnp.where(slot < cnt[0, 0], -STEP_SIZE, 0.0).astype(f32)
        for part, g in enumerate((gr, gi)):
            wide = jnp.concatenate([g * weight, jnp.zeros((SUBLANES, frame), f32)], axis=0)
            wide = pltpu.roll(wide, lift, axis=0)
            wide = jnp.concatenate([wide, jnp.zeros_like(wide)], axis=1)
            padded[slot, part, pl.ds(tall, tall), pl.ds(LANES, 2 * LANES)] = pltpu.roll(wide, rest, axis=1)

    def pair(i, carry):
        g0 = contribution(2 * i)
        g1 = contribution(2 * i + 1)
        keep_padded(2 * i, *g0)
        keep_padded(2 * i + 1, *g1)
        return carry

    lax.fori_loop(0, slots // 2, pair, 0)

    for j in (2, 3):
        for up, r in ((-1, 0), (1, 1)):
            @pl.when(jnp.logical_and(flags[r], flags[j]))
            def _():
                corner_copy(j, up).wait_send()

    places = [place_of(s) for s in range(slots)]

    def block_sum(part, j, t, total):
        for s in range(slots):
            top, _, q, _ = places[s]
            start = jnp.clip(tall // SUBLANES + j * (frame // SUBLANES) - top, 0, 2 * tall // SUBLANES) * SUBLANES
            lane = jnp.clip(t - q + 1, 0, 3) * LANES
            piece = padded[
                s, part, pl.ds(start, frame),
                pl.ds(lane, LANES),
            ]
            total = piece if total is None else total + piece
        return total

    n_lane = width // LANES + 2

    def rows_of(j, carry):
        r = pl.multiple_of(j * frame, frame)
        for part in range(2):
            for t in range(n_lane):
                where = (part, pl.ds(r, frame), pl.ds(t * LANES, LANES))
                edge = t in (0, n_lane - 1)
                win[where] = block_sum(part, j, t, None if edge else jnp.where(inner(j), win[where], 0.0))
        return carry

    lane_id = lax.broadcasted_iota(jnp.int32, (frame, LANES), 1)
    row_id = lax.broadcasted_iota(jnp.int32, (frame, LANES), 0)

    def inner(j):
        r = row_id + j * frame
        return jnp.logical_and(r >= MARGIN, r < MARGIN + height)

    lax.fori_loop(0, (height + 2 * MARGIN) // frame, rows_of, 0)

    for i in range(2):
        rim_row[i] = win[:, bands[2 * i], strips[1]]
    low = lax.broadcasted_iota(jnp.int32, (height + 2 * MARGIN, LANES), 1) < MARGIN
    every = pl.ds(0, height + 2 * MARGIN)
    re, im = win[0, every, strips[0]], win[1, every, strips[0]]
    strip[0] = jnp.where(low, pltpu.roll(re, MARGIN, axis=1), im)
    re, im = win[0, every, strips[2]], win[1, every, strips[2]]
    strip[1] = jnp.where(low, re, pltpu.roll(im, MARGIN, axis=1))

    parts, places_to = [], []
    for a, b in DIRS:
        if b == 0:
            parts.append(rim_row.at[(a + 1) // 2])
            places_to.append(got_row.at[(a + 1) // 2])
        elif a == 0:
            parts.append(strip.at[(b + 1) // 2, bands[1]])
            places_to.append(got_strip.at[(b + 1) // 2])
        else:
            parts.append(strip.at[(b + 1) // 2, bands[a + 1]])
            places_to.append(got_corner.at[(a + 1) + (b + 1) // 2])
    rims = rim_copies(parts, places_to, rsend, rrecv)
    for i in range(len(DIRS)):
        @pl.when(flags[i])
        def _():
            rims[i].start()

    out[...] = win[:, bands[1], strips[1]]

    def add_packed(value, b, r0, n):
        turned = pltpu.roll(value, MARGIN, axis=1)
        first = lax.broadcasted_iota(jnp.int32, (n, LANES), 1) < MARGIN
        if b < 0:
            c0, re, im, here = width - LANES, turned, value, jnp.logical_not(first)
        else:
            c0, re, im, here = 0, value, turned, first
        for part, v in enumerate((re, im)):
            where = (part, pl.ds(r0, n), pl.ds(c0, LANES))
            out[where] = out[where] + jnp.where(here, v, 0.0)

    for i, (a, b) in enumerate(DIRS):
        @pl.when(flags[OPP[i]])
        def _():
            rims[i].wait_recv()
            r0 = {-1: height - MARGIN, 0: 0, 1: 0}[a]
            if b == 0:
                where = (pl.ds(0, 2), pl.ds(r0, MARGIN), pl.ds(0, width))
                out[where] = out[where] + got_row[(a + 1) // 2]
            elif a == 0:
                add_packed(got_strip[(b + 1) // 2], b, 0, height)
            else:
                add_packed(got_corner[(a + 1) + (b + 1) // 2], b, r0, MARGIN)

    for k in range(1, modes):
        def sent(side):
            probe_copy(k, side).wait_send()
            if paired:
                forward_copy(k, side).wait_send()

        sided(sent)
    for i in range(4):
        @pl.when(flags[i])
        def _():
            side_copy(i).wait_send()
    for i in range(len(DIRS)):
        @pl.when(flags[i])
        def _():
            rims[i].wait_send()


def per_device(object_field, probe_real, probe_imag, amplitude, positions, counts):
    modes, cols = lax.axis_size("mode"), lax.axis_size("col")
    _, height, width = object_field.shape
    frame = probe_real.shape[-1]
    slots = amplitude.shape[2]
    f32 = jnp.float32
    tall = frame + SUBLANES
    tables = [jnp.asarray(t) for t in dft_tables(frame)]
    smem = pl.BlockSpec(memory_space=pltpu.SMEM)
    anym = pl.BlockSpec(memory_space=pl.ANY)
    sem = pltpu.SemaphoreType.DMA
    vmem = pltpu.VMEM
    return pl.pallas_call(
        functools.partial(step_kernel, modes, cols),
        out_shape=jax.ShapeDtypeStruct((2, height, width), f32),
        in_specs=[smem, smem] + [anym] * 8,
        out_specs=pl.BlockSpec(memory_space=vmem),
        scratch_shapes=[
            vmem((2, height + 2 * MARGIN + SUBLANES, width + 2 * LANES), f32),
            vmem((modes, 2, frame, frame), f32),
            vmem((slots, frame, frame), f32),
            vmem((slots, 2, frame, frame), f32),
            vmem((modes, slots, 2 * frame, frame), f32),
            vmem((slots, 2, 2 * tall + frame, 4 * LANES), f32),
            vmem((2, 2, MARGIN, width), f32),
            vmem((2, height, LANES), f32),
            vmem((4, MARGIN, LANES), f32),
            vmem((2, 2, MARGIN, width), f32),
            vmem((2, height + 2 * MARGIN, LANES), f32),
            *[vmem(t.shape, t.dtype) for t in tables],
            sem((4,)), sem((4,)),
            sem((4,)), sem((4,)),
            sem((modes - 1, 2)), sem((modes - 1, 2)),
            sem((modes - 1, 2)), sem((modes - 1, 2)),
            sem((8,)), sem((8,)),
            sem((8,)),
        ],
        compiler_params=pltpu.CompilerParams(collective_id=0, has_side_effects=True),
        name="gradient_step",
    )(jnp.swapaxes(positions, 2, 3), counts, object_field, probe_real, probe_imag, amplitude, *tables)


def solution(mesh):
    in_specs = (
        P(None, "row", "col"),
        P("mode", None, None),
        P("mode", None, None),
        P("row", "col", None, None, None),
        P("row", "col", None, None),
        P("row", "col"),
    )
    out_specs = P(None, "row", "col")
    return jax.shard_map(
        per_device, mesh=mesh, in_specs=in_specs, out_specs=out_specs, check_vma=False
    )
```

```python
import functools

import jax
import jax.numpy as jnp
import numpy as np
from jax import lax
from jax.experimental import pallas as pl
from jax.experimental.pallas import tpu as pltpu
from jax.sharding import PartitionSpec as P

MARGIN = 64
LANES = 128
SUBLANES = 8
STEP_SIZE = 0.25
MESH_ID = pl.DeviceIdType.MESH

DIRS = ((-1, 0), (1, 0), (0, -1), (0, 1), (-1, -1), (-1, 1), (1, -1), (1, 1))
OPP = tuple(DIRS.index((-a, -b)) for a, b in DIRS)


def dft_tables(length):
    k = np.arange(length)
    angle = 2.0 * np.pi * (np.outer(k, k) % length) / length
    c = np.cos(angle) / np.sqrt(length)
    s = np.sin(angle) / np.sqrt(length)
    plus = np.block([[c, s], [-s, c]])
    minus = np.block([[c, -s], [s, c]])

    def split(t):
        hi = t.astype(jnp.bfloat16)
        lo = (t - hi.astype(np.float64)).astype(jnp.bfloat16)
        return hi, lo

    ph, pw = split(plus)
    mh, mw = split(minus)
    right_f = np.concatenate([mh, mh, mw], axis=0)
    left_f = np.concatenate([ph, ph, pw], axis=1)
    left_b = np.concatenate([mh, mh, mw], axis=1)
    right_b = np.concatenate([ph, ph, pw], axis=0)
    return right_f, left_f, left_b, right_b


def neighbour_flags():
    row, col = lax.axis_index("row"), lax.axis_index("col")
    rows, cols = lax.axis_size("row"), lax.axis_size("col")
    flags = []
    for a, b in DIRS:
        r, c = row + a, col + b
        ok = jnp.logical_and(jnp.logical_and(r >= 0, r < rows), jnp.logical_and(c >= 0, c < cols))
        flags.append(ok)
    return flags


def target(step):
    return (lax.axis_index("row") + step[0], lax.axis_index("col") + step[1], lax.axis_index("mode"))


def enter(flags, others):
    barrier = pltpu.get_barrier_semaphore()
    total = jnp.int32(len(others))
    for flag, step in zip(flags, DIRS):
        total = total + flag.astype(jnp.int32)

        @pl.when(flag)
        def _():
            pl.semaphore_signal(barrier, inc=1, device_id=target(step), device_id_type=MESH_ID)

    for device in others:
        pl.semaphore_signal(barrier, inc=1, device_id=device, device_id_type=MESH_ID)
    pl.semaphore_wait(barrier, total)


def rim_copies(parts, slots, send, recv):
    return [
        pltpu.make_async_remote_copy(
            src_ref=parts[i], dst_ref=slots[i], send_sem=send.at[i], recv_sem=recv.at[i],
            device_id=target(DIRS[i]), device_id_type=MESH_ID,
        )
        for i in range(len(DIRS))
    ]


def split(x):
    hi = x.astype(jnp.bfloat16)
    lo = (x - hi.astype(jnp.float32)).astype(jnp.bfloat16)
    return hi, lo


def apply_right(x, table):
    hi, lo = split(x)
    return jnp.dot(
        jnp.concatenate([hi, lo, hi], axis=1), table, preferred_element_type=jnp.float32
    )


def apply_left(table, x):
    hi, lo = split(x)
    return jnp.dot(
        table, jnp.concatenate([hi, lo, hi], axis=0), preferred_element_type=jnp.float32
    )


def step_kernel(
    modes, cols, pos, cnt, obj, pr, pi, amp, rf_in, lf_in, lb_in, rb_in,
    out,
    win, probe, tgt, patch, spec, padded, got_row, got_strip, got_corner, rim_row, strip,
    rf, lf, lb, rb,
    send, recv, csend, crecv, psend, precv, fsend, frecv, rsend, rrecv, local,
):
    row, col, mode = lax.axis_index("row"), lax.axis_index("col"), lax.axis_index("mode")
    height, width = obj.shape[1], obj.shape[2]
    frame = pr.shape[-1]
    slots = amp.shape[2]
    tall = frame + SUBLANES
    flags = neighbour_flags()
    parity = col % 2
    paired = cols % 2 == 0
    partner = col + 1 - 2 * parity
    peers = [(row, col, (mode + k) % modes) for k in range(1, modes)]
    f32 = jnp.float32

    bands = (pl.ds(0, MARGIN), pl.ds(MARGIN, height), pl.ds(MARGIN + height, MARGIN))
    strips = (pl.ds(0, LANES), pl.ds(LANES, width), pl.ds(LANES + width, LANES))

    loads = [
        (obj, win.at[:, bands[1], strips[1]]),
        (pr.at[0], probe.at[0, 0]),
        (pi.at[0], probe.at[0, 1]),
        (amp.at[0, 0], tgt),
        (rf_in, rf), (lf_in, lf), (lb_in, lb), (rb_in, rb),
    ]
    loads = [pltpu.make_async_copy(a, b, local.at[i]) for i, (a, b) in enumerate(loads)]
    for copy in loads:
        copy.start()

    enter(flags, peers)

    def probe_copy(k, side):
        return pltpu.make_async_remote_copy(
            src_ref=(pr, pi)[side].at[0], dst_ref=probe.at[k, side], send_sem=psend.at[k - 1, side],
            recv_sem=precv.at[k - 1, side], device_id=peers[k - 1], device_id_type=MESH_ID,
        )

    def forward_copy(k, side):
        return pltpu.make_async_remote_copy(
            src_ref=probe.at[k, side], dst_ref=probe.at[k, side], send_sem=fsend.at[k - 1, side],
            recv_sem=frecv.at[k - 1, side], device_id=(row, partner, mode), device_id_type=MESH_ID,
        )

    def sided(action):
        for side in (0, 1):
            if paired:
                @pl.when(parity == side)
                def _():
                    action(side)
            else:
                action(side)

    for k in range(1, modes):
        sided(lambda side: probe_copy(k, side).start())

    def side_copy(i):
        a, b = DIRS[i]
        rs = {-1: pl.ds(0, MARGIN), 0: pl.ds(0, height), 1: pl.ds(height - MARGIN, MARGIN)}[a]
        cs = {-1: pl.ds(0, LANES), 0: pl.ds(0, width), 1: pl.ds(width - LANES, LANES)}[b]
        return pltpu.make_async_remote_copy(
            src_ref=obj.at[:, rs, cs], dst_ref=win.at[:, bands[1 - a], strips[1 - b]],
            send_sem=send.at[i], recv_sem=recv.at[i], device_id=target(DIRS[i]), device_id_type=MESH_ID,
        )

    def corner_copy(i, up):
        b = DIRS[i][1]
        cs = {-1: pl.ds(LANES, LANES), 1: pl.ds(width, LANES)}[b]
        rs = bands[up + 1]
        j = (i - 2) * 2 + (up + 1) // 2
        return pltpu.make_async_remote_copy(
            src_ref=win.at[:, rs, cs], dst_ref=win.at[:, rs, strips[1 - b]],
            send_sem=csend.at[j], recv_sem=crecv.at[j], device_id=target(DIRS[i]), device_id_type=MESH_ID,
        )

    for i in range(4):
        @pl.when(flags[i])
        def _():
            side_copy(i).start()

    for i, (a, b) in enumerate(DIRS):
        @pl.when(jnp.logical_not(flags[i]))
        def _():
            place = win.at[:, bands[a + 1], strips[b + 1]]
            place[...] = jnp.zeros(place.shape, f32)

    win[:, pl.ds(2 * MARGIN + height, SUBLANES), :] = jnp.zeros((2, SUBLANES, width + 2 * LANES), f32)

    def clear(s, carry):
        padded[s] = jnp.zeros(padded.shape[1:], f32)
        return carry

    lax.fori_loop(0, slots, clear, 0)

    for copy in loads:
        copy.wait()

    for i in (0, 1):
        up = DIRS[OPP[i]][0]

        @pl.when(flags[OPP[i]])
        def _():
            side_copy(i).wait_recv()

        for j in (2, 3):
            @pl.when(jnp.logical_and(flags[OPP[i]], flags[j]))
            def _():
                corner_copy(j, up).start()

    if paired:
        for k in range(1, modes):
            def relay(side):
                probe_copy(k, side).wait_recv()
                forward_copy(k, side).start()

            sided(relay)

    for i in (2, 3):
        @pl.when(flags[OPP[i]])
        def _():
            side_copy(i).wait_recv()

        for up, r in ((-1, 0), (1, 1)):
            @pl.when(jnp.logical_and(flags[OPP[i]], flags[r]))
            def _():
                corner_copy(i, up).wait_recv()

    def place_of(slot):
        a = pos[0, 0, 0, slot]
        b = pos[0, 0, 1, slot] + (LANES - MARGIN)
        q = lax.div(b, LANES)
        top = lax.div(a, SUBLANES)
        return top, a - top * SUBLANES, q, b - q * LANES

    def cut(slot, carry):
        top, lift, q, rest = place_of(slot)
        shift = (2 * LANES - rest) % (2 * LANES)
        for part in range(2):
            wide = win[part, pl.ds(top * SUBLANES, tall), pl.ds(q * LANES, 2 * LANES)]
            wide = pltpu.roll(wide, shift, axis=1)[:, :frame]
            patch[slot, part] = pltpu.roll(wide, (tall - lift) % tall, axis=0)[:frame]
        return carry

    lax.fori_loop(0, slots, cut, 0)

    group = min(slots, 4)

    def forward(k):
        p, q = probe[k, 0], probe[k, 1]
        groups = []
        for g in range(0, slots, group):
            waves = []
            for j in range(g, g + group):
                re, im = patch[j, 0], patch[j, 1]
                waves.append(jnp.concatenate([p * re - q * im, p * im + q * re], axis=1))
            groups.append(apply_right(jnp.concatenate(waves, axis=0), rf[...]))
        for g, z in zip(range(0, slots, group), groups):
            z = jnp.concatenate(
                [
                    jnp.concatenate([z[j * frame:(j + 1) * frame, :frame] for j in range(group)], axis=1),
                    jnp.concatenate([z[j * frame:(j + 1) * frame, frame:] for j in range(group)], axis=1),
                ],
                axis=0,
            )
            y = apply_left(lf[...], z)
            for j in range(group):
                spec[k, g + j] = y[:, j * frame:(j + 1) * frame]

    for k in range(modes):
        if k:
            if paired:
                sided(lambda side: forward_copy(k, 1 - side).wait_recv())
            else:
                sided(lambda side: probe_copy(k, side).wait_recv())
        forward(k)

    def contribution(slot):
        y = jnp.concatenate([spec[m, slot] for m in range(modes)], axis=1)
        power = y[:frame] * y[:frame] + y[frame:] * y[frame:]
        intensity = power[:, :frame]
        for m in range(1, modes):
            intensity = intensity + power[:, m * frame:(m + 1) * frame]
        keep = 1.0 - tgt[slot] / jnp.maximum(jnp.sqrt(intensity), 1.0)
        keep = jnp.concatenate([keep] * modes, axis=1)
        keep = jnp.concatenate([keep] * 2, axis=0)
        back = apply_left(lb[...], y * keep)
        back = jnp.concatenate(
            [
                jnp.concatenate(
                    [back[:frame, m * frame:(m + 1) * frame], back[frame:, m * frame:(m + 1) * frame]],
                    axis=1,
                )
                for m in range(modes)
            ],
            axis=0,
        )
        back = apply_right(back, rb[...])
        gr = jnp.zeros((frame, frame), f32)
        gi = jnp.zeros((frame, frame), f32)
        for m in range(modes):
            p, q = probe[m, 0], probe[m, 1]
            br = back[m * frame:(m + 1) * frame, :frame]
            bi = back[m * frame:(m + 1) * frame, frame:]
            gr = gr + (p * br + q * bi)
            gi = gi + (p * bi - q * br)
        return gr, gi

    def keep_padded(slot, gr, gi):
        _, lift, _, rest = place_of(slot)
        weight = jnp.where(slot < cnt[0, 0], -STEP_SIZE, 0.0).astype(f32)
        for part, g in enumerate((gr, gi)):
            wide = jnp.concatenate([g * weight, jnp.zeros((SUBLANES, frame), f32)], axis=0)
            wide = pltpu.roll(wide, lift, axis=0)
            wide = jnp.concatenate([wide, jnp.zeros_like(wide)], axis=1)
            padded[slot, part, pl.ds(tall, tall), pl.ds(LANES, 2 * LANES)] = pltpu.roll(wide, rest, axis=1)

    def some(i, carry):
        found = [contribution(group * i + j) for j in range(group)]
        for j, g in enumerate(found):
            keep_padded(group * i + j, *g)
        return carry

    lax.fori_loop(0, slots // group, some, 0)

    for j in (2, 3):
        for up, r in ((-1, 0), (1, 1)):
            @pl.when(jnp.logical_and(flags[r], flags[j]))
            def _():
                corner_copy(j, up).wait_send()

    places = [place_of(s) for s in range(slots)]

    def block_sum(part, j, t, total):
        for s in range(slots):
            top, _, q, _ = places[s]
            start = jnp.clip(tall // SUBLANES + j * (frame // SUBLANES) - top, 0, 2 * tall // SUBLANES) * SUBLANES
            lane = jnp.clip(t - q + 1, 0, 3) * LANES
            piece = padded[
                s, part, pl.ds(start, frame),
                pl.ds(lane, LANES),
            ]
            total = piece if total is None else total + piece
        return total

    n_lane = width // LANES + 2

    def rows_of(j, carry):
        r = pl.multiple_of(j * frame, frame)
        for part in range(2):
            for t in range(n_lane):
                where = (part, pl.ds(r, frame), pl.ds(t * LANES, LANES))
                edge = t in (0, n_lane - 1)
                win[where] = block_sum(part, j, t, None if edge else jnp.where(inner(j), win[where], 0.0))
        return carry

    lane_id = lax.broadcasted_iota(jnp.int32, (frame, LANES), 1)
    row_id = lax.broadcasted_iota(jnp.int32, (frame, LANES), 0)

    def inner(j):
        r = row_id + j * frame
        return jnp.logical_and(r >= MARGIN, r < MARGIN + height)

    lax.fori_loop(0, (height + 2 * MARGIN) // frame, rows_of, 0)

    for i in range(2):
        rim_row[i] = win[:, bands[2 * i], strips[1]]
    low = lax.broadcasted_iota(jnp.int32, (height + 2 * MARGIN, LANES), 1) < MARGIN
    every = pl.ds(0, height + 2 * MARGIN)
    re, im = win[0, every, strips[0]], win[1, every, strips[0]]
    strip[0] = jnp.where(low, pltpu.roll(re, MARGIN, axis=1), im)
    re, im = win[0, every, strips[2]], win[1, every, strips[2]]
    strip[1] = jnp.where(low, re, pltpu.roll(im, MARGIN, axis=1))

    parts, places_to = [], []
    for a, b in DIRS:
        if b == 0:
            parts.append(rim_row.at[(a + 1) // 2])
            places_to.append(got_row.at[(a + 1) // 2])
        elif a == 0:
            parts.append(strip.at[(b + 1) // 2, bands[1]])
            places_to.append(got_strip.at[(b + 1) // 2])
        else:
            parts.append(strip.at[(b + 1) // 2, bands[a + 1]])
            places_to.append(got_corner.at[(a + 1) + (b + 1) // 2])
    rims = rim_copies(parts, places_to, rsend, rrecv)
    for i in range(len(DIRS)):
        @pl.when(flags[i])
        def _():
            rims[i].start()

    out[...] = win[:, bands[1], strips[1]]

    def add_packed(value, b, r0, n):
        turned = pltpu.roll(value, MARGIN, axis=1)
        first = lax.broadcasted_iota(jnp.int32, (n, LANES), 1) < MARGIN
        if b < 0:
            c0, re, im, here = width - LANES, turned, value, jnp.logical_not(first)
        else:
            c0, re, im, here = 0, value, turned, first
        for part, v in enumerate((re, im)):
            where = (part, pl.ds(r0, n), pl.ds(c0, LANES))
            out[where] = out[where] + jnp.where(here, v, 0.0)

    for i, (a, b) in enumerate(DIRS):
        @pl.when(flags[OPP[i]])
        def _():
            rims[i].wait_recv()
            r0 = {-1: height - MARGIN, 0: 0, 1: 0}[a]
            if b == 0:
                where = (pl.ds(0, 2), pl.ds(r0, MARGIN), pl.ds(0, width))
                out[where] = out[where] + got_row[(a + 1) // 2]
            elif a == 0:
                add_packed(got_strip[(b + 1) // 2], b, 0, height)
            else:
                add_packed(got_corner[(a + 1) + (b + 1) // 2], b, r0, MARGIN)

    for k in range(1, modes):
        def sent(side):
            probe_copy(k, side).wait_send()
            if paired:
                forward_copy(k, side).wait_send()

        sided(sent)
    for i in range(4):
        @pl.when(flags[i])
        def _():
            side_copy(i).wait_send()
    for i in range(len(DIRS)):
        @pl.when(flags[i])
        def _():
            rims[i].wait_send()


def per_device(object_field, probe_real, probe_imag, amplitude, positions, counts):
    modes, cols = lax.axis_size("mode"), lax.axis_size("col")
    _, height, width = object_field.shape
    frame = probe_real.shape[-1]
    slots = amplitude.shape[2]
    f32 = jnp.float32
    tall = frame + SUBLANES
    tables = [jnp.asarray(t) for t in dft_tables(frame)]
    smem = pl.BlockSpec(memory_space=pltpu.SMEM)
    anym = pl.BlockSpec(memory_space=pl.ANY)
    sem = pltpu.SemaphoreType.DMA
    vmem = pltpu.VMEM
    return pl.pallas_call(
        functools.partial(step_kernel, modes, cols),
        out_shape=jax.ShapeDtypeStruct((2, height, width), f32),
        in_specs=[smem, smem] + [anym] * 8,
        out_specs=pl.BlockSpec(memory_space=vmem),
        scratch_shapes=[
            vmem((2, height + 2 * MARGIN + SUBLANES, width + 2 * LANES), f32),
            vmem((modes, 2, frame, frame), f32),
            vmem((slots, frame, frame), f32),
            vmem((slots, 2, frame, frame), f32),
            vmem((modes, slots, 2 * frame, frame), f32),
            vmem((slots, 2, 2 * tall + frame, 4 * LANES), f32),
            vmem((2, 2, MARGIN, width), f32),
            vmem((2, height, LANES), f32),
            vmem((4, MARGIN, LANES), f32),
            vmem((2, 2, MARGIN, width), f32),
            vmem((2, height + 2 * MARGIN, LANES), f32),
            *[vmem(t.shape, t.dtype) for t in tables],
            sem((4,)), sem((4,)),
            sem((4,)), sem((4,)),
            sem((modes - 1, 2)), sem((modes - 1, 2)),
            sem((modes - 1, 2)), sem((modes - 1, 2)),
            sem((8,)), sem((8,)),
            sem((8,)),
        ],
        compiler_params=pltpu.CompilerParams(collective_id=0, has_side_effects=True),
        name="gradient_step",
    )(jnp.swapaxes(positions, 2, 3), counts, object_field, probe_real, probe_imag, amplitude, *tables)


def solution(mesh):
    in_specs = (
        P(None, "row", "col"),
        P("mode", None, None),
        P("mode", None, None),
        P("row", "col", None, None, None),
        P("row", "col", None, None),
        P("row", "col"),
    )
    out_specs = P(None, "row", "col")
    return jax.shard_map(
        per_device, mesh=mesh, in_specs=in_specs, out_specs=out_specs, check_vma=False
    )
```
